32 devices in a mesh: st: 8 (over z, x), gr: 4 (over y, core).
Axes of the slice: x: 2, y: 2, z: 4, core: 2. Of those that a mesh axis runs over, the one named last changes fastest.
Arguments:
- states: float32 [32, 24, 768], P(('st', 'gr')), may hold values from -6 to 6
- regions: int32 [24, 768], replicated, may hold values from 0 to 7
- pot_table: float32 [8], replicated, may hold values from -3 to 0
- subspace: bfloat16 [32, 32], P(None, 'st'), may hold values from -1.5 to 1.5
- state_order: int32 [32], replicated, may hold values from 0 to 31, each once
Outputs:
- rotated: bfloat16 [32, 24, 768], P('st', 'gr')
The draws below stay inside these ranges and needn't reach their ends.
Inputs may be any that keep to these rules, and one draw needn't show every extreme that they name: state_order is a permutation of the window positions.
All inputs are finite; a program needn't handle non-finite values.
Results may differ from the reference program's by a relative error of at most 0.0049.
Values may be sent and summed in bfloat16 or wider, within the bound.
No kernel may reach another device: no remote copies, remote signals or barrier semaphores. Data moves between devices by JAX's collectives and lax.ppermute only.
A program may use at most 64 MiB of HBM per device.

```python
import jax
import jax.numpy as jnp
from jax import lax

NX = 24
NY = 24
NZ = 32
DEG = 4
REGIONS = 8
W = 32


def plant(values, stream_key, smallest, top_value):
    dims = values.shape
    index_at = [jax.random.randint(jax.random.fold_in(stream_key, axis), (), 0, dims[axis]) for axis in range(len(dims))]
    values = values.at[tuple(index_at)].set(smallest)
    longest = dims.index(max(dims))
    index_at[longest] = (index_at[longest] + 1) % dims[longest]
    return values.at[tuple(index_at)].set(top_value)


def spiked(entries, rng, source, target, parts, factor):
    owner, partner = [(jnp.arange(entries.shape[position]) // (entries.shape[position] // parts)).reshape([-1 if axis == position else 1 for axis in range(entries.ndim)]) for position in (source, target)]
    chosen = jax.random.permutation(rng, parts)[partner]
    strong = (owner == chosen) | (owner == (partner + parts // 2) % parts)
    return jnp.where(strong, factor * entries, entries)


def steps_of(rng, dims, split, low, high):
    level, own = 1.0, jax.random.fold_in(rng, 6)
    for axis_at, shards_of in split:
        draws = jnp.exp(jax.random.uniform(jax.random.fold_in(own, axis_at), (shards_of,), jnp.float32, low / len(split), high / len(split)))
        level = level * jnp.repeat(draws, dims[axis_at] // shards_of).reshape([-1 if axis == axis_at else 1 for axis in range(len(dims))])
    return level


def gaussian(key, extent, spread, limit, cuts=(), kind=jnp.bfloat16):
    values = jax.random.normal(key, extent, jnp.float32) * spread
    if len(cuts) > 0:
        values = steps_of(key, extent, cuts, -0.22, 0.18) * values
    return jnp.clip(values, min=-limit, max=limit).astype(kind)


def noise_with(rng, shape, spread, reach, shards, heavy, held_as=jnp.bfloat16):
    values = spread * jax.random.normal(rng, shape, jnp.float32)
    if shards:
        values = values * steps_of(rng, shape, shards, -0.22, 0.18)
    return jnp.clip(spiked(values, jax.random.fold_in(rng, 3), *heavy), -reach, reach).astype(held_as)


def setup_inputs(seed: int = 0) -> dict:
    splits = jax.random.split(jax.random.key(seed), 6)
    return {
        "states": gaussian(splits[0], (W, NX, NY * NZ), 1.0, 6.0, ((0, 32),), jnp.float32),
        "regions": plant(jax.random.randint(splits[1], (NX, NY * NZ), 0, REGIONS), jax.random.fold_in(splits[1], 1), 0, REGIONS - 1).astype(jnp.int32),
        "pot_table": jnp.clip(jax.random.uniform(splits[2], (REGIONS,), jnp.float32, -3.0, 0.0), -3.0, 0.0),
        "subspace": noise_with(splits[3], (W, W), W ** -0.5, 1.5, ((1, 8),), (0, 1, 8, 2.0)),
        "state_order": jax.random.permutation(splits[4], W).astype(jnp.int32),
    }


coef_center = -5369.0 / 1800.0
coef_list = (12.0 / 7.0, -15.0 / 56.0, 10.0 / 189.0, -1.0 / 112.0, 2.0 / 1925.0, -1.0 / 16632.0)
centre = 6.75
half_width = 5.25


def laplace(cube):
    nx, ny, nz = cube.shape
    padded = jnp.pad(cube, 6)
    total = 3.0 * coef_center * cube
    for step in range(1, 7):
        xpair = padded[6 + step:6 + step + nx, 6:6 + ny, 6:6 + nz] + padded[6 - step:6 - step + nx, 6:6 + ny, 6:6 + nz]
        ypair = padded[6:6 + nx, 6 + step:6 + step + ny, 6:6 + nz] + padded[6:6 + nx, 6 - step:6 - step + ny, 6:6 + nz]
        zpair = padded[6:6 + nx, 6:6 + ny, 6 + step:6 + step + nz] + padded[6:6 + nx, 6:6 + ny, 6 - step:6 - step + nz]
        total = total + coef_list[step - 1] * ((xpair + ypair) + zpair)
    return total


def shifted_op(cube, potential):
    return (-0.5 * laplace(cube) + potential * cube) - centre * cube


def filter_state(cube, potential):
    previous = cube
    current = shifted_op(cube, potential) * (1.0 / half_width)
    for step in range(1, DEG):
        following = shifted_op(current, potential) * (2.0 / half_width) - previous
        previous = current
        current = following
    return current


def reference(states, regions, pot_table, subspace, state_order):
    potential = pot_table[regions].reshape(NX, NY, NZ)

    def single(state):
        cube = filter_state(state.reshape(NX, NY, NZ), potential)
        return cube.reshape(NX, NY * NZ).astype(jnp.bfloat16)

    filtered = lax.map(single, states)
    weights = subspace[state_order.astype(jnp.int32)]
    rotated = jnp.dot(weights.T, filtered.reshape(W, NX * NY * NZ), preferred_element_type=jnp.float32)
    return rotated.reshape(W, NX, NY * NZ).astype(jnp.bfloat16)
```

```python
import functools

import jax
import jax.numpy as jnp
from jax import lax
from jax.experimental import pallas as pl
from jax.experimental.pallas import tpu as pltpu
from jax.sharding import PartitionSpec as P

NZ = 32
DEG = 4
LANES = 128

coef_center = -5369.0 / 1800.0
coef_list = (12.0 / 7.0, -15.0 / 56.0, 10.0 / 189.0, -1.0 / 112.0, 2.0 / 1925.0, -1.0 / 16632.0)
centre = 6.75
half_width = 5.25


def roll(value, shift, axis):
    size = value.shape[axis]
    shift = shift % size
    return value if shift == 0 else pltpu.roll(value, shift, axis)


def scaled_op(tiles, diagonal, zmasks, lane, row):
    count = len(tiles)
    height = tiles[0].shape[0]
    per_tile = LANES // NZ
    zero = jnp.zeros_like(tiles[0])
    turned = [[roll(t, NZ * k, 1) for k in range(per_tile)] for t in tiles]

    def at(k, t):
        return turned[t][k] if 0 <= t < count else zero

    result = []
    for t, tile in enumerate(tiles):
        total = diagonal[t] * tile
        for step in range(1, len(coef_list) + 1):
            weight = -0.5 * coef_list[step - 1] / half_width
            up = jnp.where(row < height - step, roll(tile, -step, 0), 0.0)
            down = jnp.where(row >= step, roll(tile, step, 0), 0.0)
            whole, part = divmod(step, per_tile)
            if part == 0:
                right, left = at(0, t + whole), at(0, t - whole)
            else:
                edge = LANES - NZ * part
                other = per_tile - part
                right = jnp.where(lane < edge, at(other, t + whole), at(other, t + whole + 1))
                left = jnp.where(lane >= NZ * part, at(part, t - whole), at(part, t - whole - 1))
            total = total + weight * ((up + down) + (right + left))
            plus, minus = zmasks[step - 1]
            total = total + (plus * roll(tile, -step, 1) + minus * roll(tile, step, 1))
        result.append(total)
    return result


def filter_kernel(table_ref, state_ref, regions_ref, out_ref):
    height, width = regions_ref.shape
    count = width // LANES
    levels = table_ref.shape[0]
    copies, groups = out_ref.shape[0], out_ref.shape[1]
    slab = height // groups
    shape = (height, LANES)
    lane = lax.broadcasted_iota(jnp.int32, shape, 1)
    row = lax.broadcasted_iota(jnp.int32, shape, 0)
    zpos = lane % NZ
    zmasks = []
    for step in range(1, len(coef_list) + 1):
        weight = -0.5 * coef_list[step - 1] / half_width
        zmasks.append(
            (jnp.where(zpos + step < NZ, weight, 0.0), jnp.where(zpos - step >= 0, weight, 0.0))
        )
    diagonal, previous = [], []
    for t in range(count):
        window = slice(t * LANES, (t + 1) * LANES)
        region = regions_ref[:, window]
        potential = jnp.zeros(shape, jnp.float32)
        for level in range(levels):
            potential = jnp.where(region == level, table_ref[level], potential)
        diagonal.append((potential - (centre + 1.5 * coef_center)) * (1.0 / half_width))
        previous.append(state_ref[0, :, window])
    current = scaled_op(previous, diagonal, zmasks, lane, row)
    for _ in range(1, DEG):
        applied = scaled_op(current, diagonal, zmasks, lane, row)
        following = [2.0 * a - p for a, p in zip(applied, previous)]
        previous, current = current, following
    for g in range(groups):
        for t in range(count):
            piece = current[t][g * slab : (g + 1) * slab].astype(jnp.bfloat16)
            for c in range(copies):
                out_ref[c, g, t * slab : (t + 1) * slab, :] = piece


def rotate_kernel(order_ref, weights_ref, blocks_ref, out_ref):
    states = blocks_ref.shape[0]
    slab, columns, width = out_ref.shape
    shape = blocks_ref.shape[1:]

    def body(s, totals):
        block = blocks_ref[s].astype(jnp.float32)
        base = order_ref[s] * columns
        return tuple(total + weights_ref[base + j] * block for j, total in enumerate(totals))

    unroll = 8 if states % 8 == 0 else 1
    totals = lax.fori_loop(
        0, states, body, tuple(jnp.zeros(shape, jnp.float32) for _ in range(columns)), unroll=unroll
    )
    for j in range(columns):
        for t in range(width // LANES):
            out_ref[:, j, t * LANES : (t + 1) * LANES] = totals[j][t * slab : (t + 1) * slab].astype(out_ref.dtype)


def grant(array):
    return 3 * array.size * array.dtype.itemsize + (4 << 20)


def per_device(st, gr, states, regions, pot_table, subspace, state_order):
    height, width = regions.shape
    slab = height // gr
    rows = slab * width // LANES
    columns = subspace.shape[1]
    vmem, smem = pl.BlockSpec(memory_space=pltpu.VMEM), pl.BlockSpec(memory_space=pltpu.SMEM)
    filtered = jax.ShapeDtypeStruct((st, gr, rows, LANES), jnp.bfloat16)
    outgoing = pl.pallas_call(
        filter_kernel,
        out_shape=filtered,
        in_specs=[smem, vmem, vmem],
        out_specs=vmem,
    )(pot_table, states, regions)
    blocks = lax.all_to_all(
        outgoing.reshape(st * gr, rows, LANES), ("st", "gr"), split_axis=0, concat_axis=0, tiled=True
    )
    weights = subspace.astype(jnp.float32).reshape(-1)
    rotated = pl.pallas_call(
        rotate_kernel,
        out_shape=jax.ShapeDtypeStruct((slab, columns, width), jnp.bfloat16),
        in_specs=[smem, smem, vmem],
        out_specs=vmem,
        compiler_params=pltpu.CompilerParams(vmem_limit_bytes=grant(blocks)),
    )(state_order, weights, blocks)
    return rotated.transpose(1, 0, 2)


def solution(mesh):
    in_specs = (P(("st", "gr"), None, None), P(), P(), P(None, "st"), P())
    out_specs = P("st", "gr", None)
    body = functools.partial(per_device, mesh.shape["st"], mesh.shape["gr"])
    return jax.shard_map(body, mesh=mesh, in_specs=in_specs, out_specs=out_specs, check_vma=False)
```

```python
import functools

import jax
import jax.numpy as jnp
from jax import lax
from jax.experimental import pallas as pl
from jax.experimental.pallas import tpu as pltpu
from jax.sharding import PartitionSpec as P

NZ = 32
DEG = 4
LANES = 128

coef_center = -5369.0 / 1800.0
coef_list = (12.0 / 7.0, -15.0 / 56.0, 10.0 / 189.0, -1.0 / 112.0, 2.0 / 1925.0, -1.0 / 16632.0)
centre = 6.75
half_width = 5.25


def roll(value, shift, axis):
    size = value.shape[axis]
    shift = shift % size
    return value if shift == 0 else pltpu.roll(value, shift, axis)


def scaled_op(tiles, diagonal, zmasks, lane, row):
    count = len(tiles)
    height = tiles[0].shape[0]
    per_tile = LANES // NZ
    zero = jnp.zeros_like(tiles[0])
    turned = [[roll(t, NZ * k, 1) for k in range(per_tile)] for t in tiles]

    def at(k, t):
        return turned[t][k] if 0 <= t < count else zero

    result = []
    for t, tile in enumerate(tiles):
        total = diagonal[t] * tile
        for step in range(1, len(coef_list) + 1):
            weight = -0.5 * coef_list[step - 1] / half_width
            up = jnp.where(row < height - step, roll(tile, -step, 0), 0.0)
            down = jnp.where(row >= step, roll(tile, step, 0), 0.0)
            whole, part = divmod(step, per_tile)
            if part == 0:
                right, left = at(0, t + whole), at(0, t - whole)
            else:
                edge = LANES - NZ * part
                other = per_tile - part
                right = jnp.where(lane < edge, at(other, t + whole), at(other, t + whole + 1))
                left = jnp.where(lane >= NZ * part, at(part, t - whole), at(part, t - whole - 1))
            total = total + weight * ((up + down) + (right + left))
            plus, minus = zmasks[step - 1]
            total = total + (plus * roll(tile, -step, 1) + minus * roll(tile, step, 1))
        result.append(total)
    return result


def filter_kernel(
    state_hbm, regions_hbm, table_hbm, order_hbm, subspace_hbm,
    out_ref, weights_ref,
    state_ref, regions_ref, table_ref, order_ref, subspace_ref, sems,
):
    sources = (regions_hbm, table_hbm, state_hbm, order_hbm, subspace_hbm)
    targets = (regions_ref, table_ref, state_ref, order_ref, subspace_ref)
    copies = [pltpu.make_async_copy(a, b, sems.at[i]) for i, (a, b) in enumerate(zip(sources, targets))]
    for copy in copies:
        copy.start()
    height, width = regions_ref.shape
    count = width // LANES
    levels = table_ref.shape[0]
    groups = out_ref.shape[0]
    slab = height // groups
    shape = (height, LANES)
    lane = lax.broadcasted_iota(jnp.int32, shape, 1)
    row = lax.broadcasted_iota(jnp.int32, shape, 0)
    zpos = lane % NZ
    zmasks = []
    for step in range(1, len(coef_list) + 1):
        weight = -0.5 * coef_list[step - 1] / half_width
        zmasks.append(
            (jnp.where(zpos + step < NZ, weight, 0.0), jnp.where(zpos - step >= 0, weight, 0.0))
        )
    diagonal = []
    copies[0].wait()
    copies[1].wait()
    for t in range(count):
        region = regions_ref[:, t * LANES : (t + 1) * LANES]
        potential = jnp.zeros(shape, jnp.float32)
        for level in range(levels):
            potential = jnp.where(region == level, table_ref[level], potential)
        diagonal.append((potential - (centre + 1.5 * coef_center)) * (1.0 / half_width))
    copies[2].wait()
    previous = [state_ref[0, :, t * LANES : (t + 1) * LANES] for t in range(count)]
    current = scaled_op(previous, diagonal, zmasks, lane, row)
    for _ in range(1, DEG):
        applied = scaled_op(current, diagonal, zmasks, lane, row)
        following = [2.0 * a - p for a, p in zip(applied, previous)]
        previous, current = current, following
    for g in range(groups):
        for t in range(count):
            piece = current[t][g * slab : (g + 1) * slab].astype(jnp.bfloat16)
            out_ref[g, t * slab : (t + 1) * slab, :] = piece
    copies[3].wait()
    copies[4].wait()
    columns, states = subspace_ref.shape
    place = lax.broadcasted_iota(jnp.int32, (states, states), 0)
    here = lax.broadcasted_iota(jnp.int32, (states, states), 1)
    chosen = jnp.where(order_ref[...] == place, 1.0, 0.0).astype(jnp.bfloat16)
    weights = jnp.dot(subspace_ref[...], chosen, preferred_element_type=jnp.float32)
    ones = jnp.ones((states, LANES), jnp.bfloat16)
    for j in range(columns):
        spread = jnp.where(place == here, weights[j : j + 1], 0.0).astype(jnp.bfloat16)
        weights_ref[j] = jnp.dot(spread, ones, preferred_element_type=jnp.float32)


def rotate_kernel(weights_ref, blocks_ref, out_ref):
    states = blocks_ref.shape[0]
    slab, columns, width = out_ref.shape
    shape = blocks_ref.shape[1:]

    def body(s, totals):
        block = blocks_ref[s].astype(jnp.float32)
        return tuple(total + weights_ref[j, pl.ds(s, 1)] * block for j, total in enumerate(totals))

    unroll = 8 if states % 8 == 0 else 1
    totals = lax.fori_loop(
        0, states, body, tuple(jnp.zeros(shape, jnp.float32) for _ in range(columns)), unroll=unroll
    )
    for j in range(columns):
        for t in range(width // LANES):
            out_ref[:, j, t * LANES : (t + 1) * LANES] = totals[j][t * slab : (t + 1) * slab].astype(out_ref.dtype)


def grant(array):
    return 3 * array.size * array.dtype.itemsize + (4 << 20)


def per_device(st, gr, states, regions, pot_table, subspace, state_order):
    height, width = regions.shape
    slab = height // gr
    rows = slab * width // LANES
    columns = subspace.shape[1]
    hbm = pl.BlockSpec(memory_space=pltpu.HBM)
    vmem = pl.BlockSpec(memory_space=pltpu.VMEM)
    filtered = jax.ShapeDtypeStruct((gr, rows, LANES), jnp.bfloat16)
    order = state_order.reshape(1, -1)
    inputs = [pltpu.with_memory_space_constraint(a, pltpu.HBM) for a in (states, regions, pot_table, order, subspace.T)]
    spaces = (pltpu.VMEM, pltpu.VMEM, pltpu.SMEM, pltpu.VMEM, pltpu.VMEM)
    outgoing, weights = pl.pallas_call(
        filter_kernel,
        out_shape=(filtered, jax.ShapeDtypeStruct((columns, subspace.shape[0], LANES), jnp.float32)),
        in_specs=[hbm] * 5,
        out_specs=(vmem, vmem),
        scratch_shapes=[space(a.shape, a.dtype) for space, a in zip(spaces, inputs)] + [pltpu.SemaphoreType.DMA((5,))],
        compiler_params=pltpu.CompilerParams(vmem_limit_bytes=grant(filtered)),
    )(*inputs)
    blocks = lax.all_to_all(
        jnp.broadcast_to(outgoing, (st, gr, rows, LANES)).reshape(st * gr, rows, LANES), ("st", "gr"), split_axis=0, concat_axis=0, tiled=True
    )
    rotated = pl.pallas_call(
        rotate_kernel,
        out_shape=jax.ShapeDtypeStruct((slab, columns, width), jnp.bfloat16),
        in_specs=[vmem, vmem],
        out_specs=vmem,
        compiler_params=pltpu.CompilerParams(vmem_limit_bytes=grant(blocks)),
    )(weights, blocks)
    return rotated.transpose(1, 0, 2)


def solution(mesh):
    in_specs = (P(("st", "gr"), None, None), P(), P(), P(None, "st"), P())
    out_specs = P("st", "gr", None)
    body = functools.partial(per_device, mesh.shape["st"], mesh.shape["gr"])
    return jax.shard_map(body, mesh=mesh, in_specs=in_specs, out_specs=out_specs, check_vma=False)
```

```python
import functools
import math

import jax
import jax.numpy as jnp
import numpy as np
from jax import lax
from jax.experimental import pallas as pl
from jax.experimental.pallas import tpu as pltpu
from jax.sharding import PartitionSpec as P

NZ = 32
DEG = 4
LANES = 128

coef_center = -5369.0 / 1800.0
coef_list = (12.0 / 7.0, -15.0 / 56.0, 10.0 / 189.0, -1.0 / 112.0, 2.0 / 1925.0, -1.0 / 16632.0)
centre = 6.75
half_width = 5.25


weight_list = tuple(-0.5 * c / half_width for c in coef_list)


def halves(level):
    high = float(np.float32(weight_list[level]).astype(jnp.bfloat16))
    return high, weight_list[level] - high


def banded(distance, allowed, part):
    matrix = jnp.zeros(distance.shape, jnp.float32)
    for level in range(len(weight_list)):
        matrix = jnp.where(distance == level + 1, halves(level)[part], matrix)
    return jnp.where(allowed, matrix, 0.0).astype(jnp.bfloat16)


def in_tile_matrix(part):
    shape = (LANES, LANES)
    source = lax.broadcasted_iota(jnp.int32, shape, 0)
    target = lax.broadcasted_iota(jnp.int32, shape, 1)
    along_z = banded(abs(source - target), source // NZ == target // NZ, part)
    along_y = banded(abs(source // NZ - target // NZ), source % NZ == target % NZ, part)
    return along_z + along_y


def row_matrix(height, padded):
    shape = (padded, padded)
    target = lax.broadcasted_iota(jnp.int32, shape, 0)
    source = lax.broadcasted_iota(jnp.int32, shape, 1)
    high, low = (banded(abs(source - target), source < height, part) for part in (0, 1))
    return jnp.concatenate([high, high, low], axis=1)


def tile_couplings(shape):
    group = lax.broadcasted_iota(jnp.int32, shape, 1) // NZ
    per_tile, reach = LANES // NZ, len(weight_list)
    couplings = {}
    for away in range(-(reach // per_tile) - 1, reach // per_tile + 2):
        if away == 0:
            continue
        for turn in range(per_tile):
            steps = [abs(per_tile * away + (g - turn) % per_tile - g) for g in range(per_tile)]
            if min(steps) > reach:
                continue
            factor = jnp.zeros(shape, jnp.float32)
            for g, step in enumerate(steps):
                if step <= reach:
                    factor = jnp.where(group == g, weight_list[step - 1], factor)
            couplings[away, turn] = factor
    return couplings


def scaled_op(tiles, diagonal, rows_matrix, lanes_matrix, couplings):
    count = len(tiles)
    height = tiles[0].shape[0]
    padded = rows_matrix.shape[0]
    blank = jnp.zeros((padded - height, LANES), jnp.float32)
    highs, lows = [], []
    for tile in tiles:
        high = tile.astype(jnp.bfloat16)
        low = tile - high.astype(jnp.float32)
        highs.append(jnp.concatenate([tile, blank], axis=0).astype(jnp.bfloat16))
        lows.append(jnp.concatenate([low, blank], axis=0).astype(jnp.bfloat16))
    pairs = jnp.concatenate([jnp.concatenate([h, l], axis=1) for h, l in zip(highs, lows)], axis=0)
    along_lanes = jnp.dot(pairs, lanes_matrix, preferred_element_type=jnp.float32)
    high_row, low_row = jnp.concatenate(highs, axis=1), jnp.concatenate(lows, axis=1)
    along_rows = jnp.dot(
        rows_matrix, jnp.concatenate([high_row, low_row, high_row], axis=0), preferred_element_type=jnp.float32
    )
    turned = [
        [t if k == 0 else pltpu.roll(t, NZ * k, 1) for k in range(LANES // NZ)] for t in tiles
    ]
    result = []
    for t, tile in enumerate(tiles):
        total = diagonal[t] * tile
        for (away, turn), factor in couplings.items():
            if 0 <= t + away < count:
                total = total + factor * turned[t + away][turn]
        lanes_part = along_lanes[t * padded : t * padded + height]
        rows_part = along_rows[:height, t * LANES : (t + 1) * LANES]
        result.append(total + (rows_part + (lanes_part[:, :LANES] + lanes_part[:, LANES:])))
    return result


def filter_kernel(
    slab,
    state_hbm, regions_hbm, table_hbm, order_hbm, subspace_hbm,
    out_ref, weights_ref,
    state_ref, regions_ref, table_ref, order_ref, subspace_ref, lanes_ref, sems,
):
    sources = (regions_hbm, table_hbm, state_hbm, order_hbm, subspace_hbm)
    targets = (regions_ref, table_ref, state_ref, order_ref, subspace_ref)
    copies = [pltpu.make_async_copy(a, b, sems.at[i]) for i, (a, b) in enumerate(zip(sources, targets))]
    for copy in copies:
        copy.start()
    height, width = regions_ref.shape
    count = width // LANES
    levels = table_ref.shape[0]
    shape = (height, LANES)
    high = in_tile_matrix(0)
    lanes_ref[:LANES, :LANES] = high
    lanes_ref[LANES:, :LANES] = high
    lanes_ref[:LANES, LANES:] = in_tile_matrix(1)
    lanes_ref[LANES:, LANES:] = jnp.zeros((LANES, LANES), jnp.bfloat16)
    rows_matrix = row_matrix(height, -(-height // 16) * 16)
    couplings = tile_couplings(shape)
    diagonal = []
    copies[0].wait()
    copies[1].wait()
    for t in range(count):
        region = regions_ref[:, t * LANES : (t + 1) * LANES]
        potential = jnp.zeros(shape, jnp.float32)
        for level in range(levels):
            potential = jnp.where(region == level, table_ref[level], potential)
        diagonal.append((potential - (centre + 1.5 * coef_center)) * (1.0 / half_width))
    copies[2].wait()
    previous = [state_ref[0, :, t * LANES : (t + 1) * LANES] for t in range(count)]
    current = scaled_op(previous, diagonal, rows_matrix, lanes_ref[...], couplings)
    for _ in range(1, DEG):
        applied = scaled_op(current, diagonal, rows_matrix, lanes_ref[...], couplings)
        following = [2.0 * a - p for a, p in zip(applied, previous)]
        previous, current = current, following
    pieces = [tile[at : at + slab] for at in range(0, height, slab) for tile in current]
    out_ref[...] = jnp.concatenate(pieces, axis=0).astype(jnp.bfloat16)
    copies[3].wait()
    copies[4].wait()
    columns, states = subspace_ref.shape
    place = lax.broadcasted_iota(jnp.int32, (states, states), 0)
    here = lax.broadcasted_iota(jnp.int32, (states, states), 1)
    chosen = jnp.where(order_ref[...] == place, 1.0, 0.0).astype(jnp.bfloat16)
    weights = jnp.dot(subspace_ref[...], chosen, preferred_element_type=jnp.float32)
    ones = jnp.ones((states, LANES), jnp.bfloat16)
    for j in range(columns):
        spread = jnp.where(place == here, weights[j : j + 1], 0.0).astype(jnp.bfloat16)
        weights_ref[j] = jnp.dot(spread, ones, preferred_element_type=jnp.float32)


def rotate_kernel(weights_ref, blocks_ref, out_ref):
    states = weights_ref.shape[1]
    slab, columns, width = out_ref.shape
    rows = slab * width // LANES
    pair = 2 * rows
    sublane = lax.broadcasted_iota(jnp.int32, (8, LANES), 0)

    def body(p, totals):
        tiles = [
            blocks_ref[pl.ds(pl.multiple_of(p * pair + 8 * i, 8), 8)].astype(jnp.float32) for i in range(pair // 8)
        ]
        result = []
        for j in range(columns):
            first = jnp.broadcast_to(weights_ref[j, pl.ds(2 * p, 1)], (8, LANES))
            second = jnp.broadcast_to(weights_ref[j, pl.ds(2 * p + 1, 1)], (8, LANES))
            for i, tile in enumerate(tiles):
                if 8 * i + 8 <= rows:
                    weight = first
                elif 8 * i >= rows:
                    weight = second
                else:
                    weight = jnp.where(sublane < rows - 8 * i, first, second)
                result.append(totals[len(result)] + weight * tile)
        return tuple(result)

    start = tuple(jnp.zeros((8, LANES), jnp.float32) for _ in range(columns * pair // 8))
    totals = lax.fori_loop(0, states // 2, body, start, unroll=4 if states % 8 == 0 else 1)
    for j in range(columns):
        both = jnp.concatenate(totals[j * (pair // 8) : (j + 1) * (pair // 8)], axis=0)
        total = both[:rows] + both[rows:]
        for t in range(width // LANES):
            out_ref[:, j, t * LANES : (t + 1) * LANES] = total[t * slab : (t + 1) * slab].astype(out_ref.dtype)


def grant(array):
    return 3 * array.size * array.dtype.itemsize + (4 << 20)


def per_device(st, gr, states, regions, pot_table, subspace, state_order):
    height, width = regions.shape
    slab = height // gr
    rows = slab * width // LANES
    columns = subspace.shape[1]
    hbm = pl.BlockSpec(memory_space=pltpu.HBM)
    vmem = pl.BlockSpec(memory_space=pltpu.VMEM)
    unit = math.gcd(rows, 8)
    chunk = (rows // unit, unit, LANES)
    filtered = jax.ShapeDtypeStruct((gr * rows, LANES), jnp.bfloat16)
    order = state_order.reshape(1, -1)
    inputs = [pltpu.with_memory_space_constraint(a, pltpu.HBM) for a in (states, regions, pot_table, order, subspace.T)]
    spaces = (pltpu.VMEM, pltpu.VMEM, pltpu.SMEM, pltpu.VMEM, pltpu.VMEM)
    outgoing, weights = pl.pallas_call(
        functools.partial(filter_kernel, slab),
        out_shape=(filtered, jax.ShapeDtypeStruct((columns, subspace.shape[0], LANES), jnp.float32)),
        in_specs=[hbm] * 5,
        out_specs=(vmem, vmem),
        scratch_shapes=[space(a.shape, a.dtype) for space, a in zip(spaces, inputs)]
        + [pltpu.VMEM((2 * LANES, 2 * LANES), jnp.bfloat16), pltpu.SemaphoreType.DMA((5,))],
        compiler_params=pltpu.CompilerParams(vmem_limit_bytes=grant(filtered)),
    )(*inputs)
    blocks = lax.all_to_all(
        jnp.broadcast_to(outgoing, (st, gr * rows, LANES)).reshape(st * gr, *chunk), ("st", "gr"), split_axis=0, concat_axis=0, tiled=True
    )
    rotated = pl.pallas_call(
        rotate_kernel,
        out_shape=jax.ShapeDtypeStruct((slab, columns, width), jnp.bfloat16),
        in_specs=[vmem, vmem],
        out_specs=vmem,
        compiler_params=pltpu.CompilerParams(vmem_limit_bytes=grant(blocks)),
    )(weights, blocks.reshape(-1, LANES))
    return rotated.transpose(1, 0, 2)


def solution(mesh):
    in_specs = (P(("st", "gr"), None, None), P(), P(), P(None, "st"), P())
    out_specs = P("st", "gr", None)
    body = functools.partial(per_device, mesh.shape["st"], mesh.shape["gr"])
    return jax.shard_map(body, mesh=mesh, in_specs=in_specs, out_specs=out_specs, check_vma=False)
```

```python
import functools
import math

import jax
import jax.numpy as jnp
import numpy as np
from jax import lax
from jax.experimental import pallas as pl
from jax.experimental.pallas import tpu as pltpu
from jax.sharding import PartitionSpec as P

NZ = 32
DEG = 4
LANES = 128

coef_center = -5369.0 / 1800.0
coef_list = (12.0 / 7.0, -15.0 / 56.0, 10.0 / 189.0, -1.0 / 112.0, 2.0 / 1925.0, -1.0 / 16632.0)
centre = 6.75
half_width = 5.25


weight_list = tuple(-0.5 * c / half_width for c in coef_list)


def halves(level):
    high = float(np.float32(weight_list[level]).astype(jnp.bfloat16))
    return high, weight_list[level] - high


def banded(distance, allowed, part):
    matrix = jnp.zeros(distance.shape, jnp.float32)
    for level in range(len(weight_list)):
        matrix = jnp.where(distance == level + 1, halves(level)[part], matrix)
    return jnp.where(allowed, matrix, 0.0).astype(jnp.bfloat16)


def in_tile_matrix(part):
    shape = (LANES, LANES)
    source = lax.broadcasted_iota(jnp.int32, shape, 0)
    target = lax.broadcasted_iota(jnp.int32, shape, 1)
    along_z = banded(abs(source - target), source // NZ == target // NZ, part)
    along_y = banded(abs(source // NZ - target // NZ), source % NZ == target % NZ, part)
    return along_z + along_y


def row_matrix(height, padded):
    shape = (padded, padded)
    target = lax.broadcasted_iota(jnp.int32, shape, 0)
    source = lax.broadcasted_iota(jnp.int32, shape, 1)
    high, low = (banded(abs(source - target), source < height, part) for part in (0, 1))
    return jnp.concatenate([high, high, low], axis=1)


def tile_couplings(shape):
    group = lax.broadcasted_iota(jnp.int32, shape, 1) // NZ
    per_tile, reach = LANES // NZ, len(weight_list)
    couplings = {}
    for away in range(-(reach // per_tile) - 1, reach // per_tile + 2):
        if away == 0:
            continue
        for turn in range(per_tile):
            steps = [abs(per_tile * away + (g - turn) % per_tile - g) for g in range(per_tile)]
            if min(steps) > reach:
                continue
            factor = jnp.zeros(shape, jnp.float32)
            for g, step in enumerate(steps):
                if step <= reach:
                    factor = jnp.where(group == g, weight_list[step - 1], factor)
            couplings[away, turn] = factor
    return couplings


def scaled_op(tiles, diagonal, rows_matrix, lanes_matrix, couplings):
    count = len(tiles)
    height = tiles[0].shape[0]
    padded = rows_matrix.shape[0]
    blank = jnp.zeros((padded - height, LANES), jnp.float32)
    highs, lows = [], []
    for tile in tiles:
        full = jnp.concatenate([tile, blank], axis=0)
        highs.append(full.astype(jnp.bfloat16))
        lows.append((full - highs[-1].astype(jnp.float32)).astype(jnp.bfloat16))
    pairs = jnp.concatenate([jnp.concatenate([h, l], axis=1) for h, l in zip(highs, lows)], axis=0)
    along_lanes = jnp.dot(pairs, lanes_matrix, preferred_element_type=jnp.float32)
    along_rows = []
    for at in range(0, count, 2):
        high_row, low_row = jnp.concatenate(highs[at : at + 2], axis=1), jnp.concatenate(lows[at : at + 2], axis=1)
        stacked = jnp.concatenate([high_row, low_row, high_row], axis=0)
        along_rows.append(jnp.dot(rows_matrix, stacked, preferred_element_type=jnp.float32))
    along_rows = jnp.concatenate(along_rows, axis=1)
    turned = [
        [t if k == 0 else pltpu.roll(t, NZ * k, 1) for k in range(LANES // NZ)] for t in tiles
    ]
    result = []
    for t, tile in enumerate(tiles):
        total = diagonal[t] * tile
        for (away, turn), factor in couplings.items():
            if 0 <= t + away < count:
                total = total + factor * turned[t + away][turn]
        lanes_part = along_lanes[t * padded : t * padded + height]
        rows_part = along_rows[:height, t * LANES : (t + 1) * LANES]
        result.append(total + (rows_part + (lanes_part[:, :LANES] + lanes_part[:, LANES:])))
    return result


def device_at(place, st, gr):
    if st % 2 or gr % 2:
        return place
    block, within = place // gr, place % gr
    st_index = st - 2 - 2 * (block // 2) + block % 2
    gr_index = 2 * (within % (gr // 2)) + 1 - within // (gr // 2)
    return st_index * gr + gr_index


def filter_kernel(
    st, gr, slab,
    state_hbm, regions_hbm, table_hbm, order_hbm, subspace_hbm,
    out_ref, weights_ref,
    state_ref, regions_ref, table_ref, order_ref, subspace_ref, lanes_ref, sems,
):
    sources = (order_hbm, subspace_hbm, table_hbm, regions_hbm, state_hbm)
    targets = (order_ref, subspace_ref, table_ref, regions_ref, state_ref)
    copies = [pltpu.make_async_copy(a, b, sems.at[i]) for i, (a, b) in enumerate(zip(sources, targets))]
    for copy in copies:
        copy.start()
    height, width = regions_ref.shape
    count = width // LANES
    levels = table_ref.shape[0]
    shape = (height, LANES)
    high = in_tile_matrix(0)
    lanes_ref[:LANES, :LANES] = high
    lanes_ref[LANES:, :LANES] = high
    lanes_ref[:LANES, LANES:] = in_tile_matrix(1)
    lanes_ref[LANES:, LANES:] = jnp.zeros((LANES, LANES), jnp.bfloat16)
    rows_matrix = row_matrix(height, -(-height // 16) * 16)
    couplings = tile_couplings(shape)
    copies[0].wait()
    copies[1].wait()
    columns, states = subspace_ref.shape
    place = lax.broadcasted_iota(jnp.int32, (states, states), 0)
    here = lax.broadcasted_iota(jnp.int32, (states, states), 1)
    chosen = jnp.where(order_ref[...] == place, 1.0, 0.0).astype(jnp.bfloat16)
    weights = jnp.dot(subspace_ref[...], chosen, preferred_element_type=jnp.float32)
    ones = jnp.ones((states, LANES), jnp.bfloat16)
    for j in range(columns):
        spread = jnp.where(device_at(place, st, gr) == here, weights[j : j + 1], 0.0).astype(jnp.bfloat16)
        weights_ref[j] = jnp.dot(spread, ones, preferred_element_type=jnp.float32)
    diagonal = []
    copies[2].wait()
    copies[3].wait()
    for t in range(count):
        region = regions_ref[:, t * LANES : (t + 1) * LANES]
        potential = jnp.zeros(shape, jnp.float32)
        for level in range(levels):
            potential = jnp.where(region == level, table_ref[level], potential)
        diagonal.append((potential - (centre + 1.5 * coef_center)) * (1.0 / half_width))
    copies[4].wait()
    previous = [state_ref[0, :, t * LANES : (t + 1) * LANES] for t in range(count)]
    current = scaled_op(previous, diagonal, rows_matrix, lanes_ref[...], couplings)
    for _ in range(1, DEG):
        applied = scaled_op(current, diagonal, rows_matrix, lanes_ref[...], couplings)
        following = [2.0 * a - p for a, p in zip(applied, previous)]
        previous, current = current, following
    slabs = [device_at(place, st, gr) % gr for place in range(gr)]
    pieces = [tile[g * slab : (g + 1) * slab] for g in slabs for tile in current]
    filtered = jnp.concatenate(pieces, axis=0).astype(jnp.bfloat16)
    size = filtered.shape[0]

    def put(copy, _):
        out_ref[pl.ds(pl.multiple_of(copy * size, 16), size)] = filtered
        return _

    copies_out = out_ref.shape[0] // size
    lax.fori_loop(0, copies_out, put, 0, unroll=math.gcd(copies_out, 8))


def rotate_kernel(weights_ref, blocks_ref, out_ref):
    states = weights_ref.shape[1]
    slab, columns, width = out_ref.shape
    rows = slab * width // LANES
    pair = 2 * rows
    sublane = lax.broadcasted_iota(jnp.int32, (8, LANES), 0)

    def body(p, totals):
        tiles = [
            blocks_ref[pl.ds(pl.multiple_of(p * pair + 8 * i, 8), 8)].astype(jnp.float32) for i in range(pair // 8)
        ]
        result = []
        for j in range(columns):
            first = jnp.broadcast_to(weights_ref[j, pl.ds(2 * p, 1)], (8, LANES))
            second = jnp.broadcast_to(weights_ref[j, pl.ds(2 * p + 1, 1)], (8, LANES))
            for i, tile in enumerate(tiles):
                if 8 * i + 8 <= rows:
                    weight = first
                elif 8 * i >= rows:
                    weight = second
                else:
                    weight = jnp.where(sublane < rows - 8 * i, first, second)
                result.append(totals[len(result)] + weight * tile)
        return tuple(result)

    start = tuple(jnp.zeros((8, LANES), jnp.float32) for _ in range(columns * pair // 8))
    totals = lax.fori_loop(0, states // 2, body, start, unroll=8 if states % 16 == 0 else 1)
    for j in range(columns):
        both = jnp.concatenate(totals[j * (pair // 8) : (j + 1) * (pair // 8)], axis=0)
        total = both[:rows] + both[rows:]
        for t in range(width // LANES):
            out_ref[:, j, t * LANES : (t + 1) * LANES] = total[t * slab : (t + 1) * slab].astype(out_ref.dtype)


def grant(array):
    return 3 * array.size * array.dtype.itemsize + (4 << 20)


def per_device(st, gr, states, regions, pot_table, subspace, state_order):
    height, width = regions.shape
    slab = height // gr
    rows = slab * width // LANES
    columns = subspace.shape[1]
    hbm = pl.BlockSpec(memory_space=pltpu.HBM)
    vmem = pl.BlockSpec(memory_space=pltpu.VMEM)
    unit = math.gcd(rows, 8)
    chunk = (rows // unit, unit, LANES)
    filtered = jax.ShapeDtypeStruct((st * gr * rows, LANES), jnp.bfloat16)
    order = state_order.reshape(1, -1)
    inputs = [pltpu.with_memory_space_constraint(a, pltpu.HBM) for a in (states, regions, pot_table, order, subspace.T)]
    spaces = (pltpu.VMEM, pltpu.VMEM, pltpu.SMEM, pltpu.VMEM, pltpu.VMEM)
    outgoing, weights = pl.pallas_call(
        functools.partial(filter_kernel, st, gr, slab),
        out_shape=(filtered, jax.ShapeDtypeStruct((columns, subspace.shape[0], LANES), jnp.float32)),
        in_specs=[hbm] * 5,
        out_specs=(vmem, vmem),
        scratch_shapes=[space(a.shape, a.dtype) for space, a in zip(spaces, inputs)]
        + [pltpu.VMEM((2 * LANES, 2 * LANES), jnp.bfloat16), pltpu.SemaphoreType.DMA((5,))],
        compiler_params=pltpu.CompilerParams(vmem_limit_bytes=grant(filtered)),
    )(*inputs)
    blocks = lax.all_to_all(
        outgoing.reshape(st * gr, *chunk),
        ("st", "gr"),
        split_axis=0,
        concat_axis=0,
        tiled=True,
        axis_index_groups=[[device_at(place, st, gr) for place in range(st * gr)]],
    )
    rotated = pl.pallas_call(
        rotate_kernel,
        out_shape=jax.ShapeDtypeStruct((slab, columns, width), jnp.bfloat16),
        in_specs=[vmem, vmem],
        out_specs=vmem,
        compiler_params=pltpu.CompilerParams(vmem_limit_bytes=grant(blocks)),
    )(weights, blocks.reshape(-1, LANES))
    return rotated.transpose(1, 0, 2)


def solution(mesh):
    in_specs = (P(("st", "gr"), None, None), P(), P(), P(None, "st"), P())
    out_specs = P("st", "gr", None)
    body = functools.partial(per_device, mesh.shape["st"], mesh.shape["gr"])
    return jax.shard_map(body, mesh=mesh, in_specs=in_specs, out_specs=out_specs, check_vma=False)
```

```python
import functools
import math

import jax
import jax.numpy as jnp
import numpy as np
from jax import lax
from jax.experimental import pallas as pl
from jax.experimental.pallas import tpu as pltpu
from jax.sharding import PartitionSpec as P

NZ = 32
DEG = 4
LANES = 128

coef_center = -5369.0 / 1800.0
coef_list = (12.0 / 7.0, -15.0 / 56.0, 10.0 / 189.0, -1.0 / 112.0, 2.0 / 1925.0, -1.0 / 16632.0)
centre = 6.75
half_width = 5.25

st_pattern = (7, 3, 5, 6, 2, 0, 4, 1)
gr_pattern = (0, 2, 3, 1)


weight_list = tuple(-0.5 * c / half_width for c in coef_list)


def halves(level):
    high = float(np.float32(weight_list[level]).astype(jnp.bfloat16))
    return high, weight_list[level] - high


def banded(distance, allowed, part):
    matrix = jnp.zeros(distance.shape, jnp.float32)
    for level in range(len(weight_list)):
        matrix = jnp.where(distance == level + 1, halves(level)[part], matrix)
    return jnp.where(allowed, matrix, 0.0).astype(jnp.bfloat16)


def in_tile_matrix(part):
    shape = (LANES, LANES)
    source = lax.broadcasted_iota(jnp.int32, shape, 0)
    target = lax.broadcasted_iota(jnp.int32, shape, 1)
    along_z = banded(abs(source - target), source // NZ == target // NZ, part)
    along_y = banded(abs(source // NZ - target // NZ), source % NZ == target % NZ, part)
    return along_z + along_y


def row_matrix(height, padded):
    shape = (padded, padded)
    target = lax.broadcasted_iota(jnp.int32, shape, 0)
    source = lax.broadcasted_iota(jnp.int32, shape, 1)
    high, low = (banded(abs(source - target), source < height, part) for part in (0, 1))
    return jnp.concatenate([high, high, low], axis=1)


def tile_couplings(shape):
    group = lax.broadcasted_iota(jnp.int32, shape, 1) // NZ
    per_tile, reach = LANES // NZ, len(weight_list)
    couplings = {}
    for away in range(-(reach // per_tile) - 1, reach // per_tile + 2):
        if away == 0:
            continue
        for turn in range(per_tile):
            steps = [abs(per_tile * away + (g - turn) % per_tile - g) for g in range(per_tile)]
            if min(steps) > reach:
                continue
            factor = jnp.zeros(shape, jnp.float32)
            for g, step in enumerate(steps):
                if step <= reach:
                    factor = jnp.where(group == g, weight_list[step - 1], factor)
            couplings[away, turn] = factor
    return couplings


def scaled_op(tiles, diagonal, rows_matrix, lanes_matrix, couplings):
    count = len(tiles)
    height = tiles[0].shape[0]
    padded = rows_matrix.shape[0]
    blank = jnp.zeros((padded - height, LANES), jnp.float32)
    highs, lows = [], []
    for tile in tiles:
        full = jnp.concatenate([tile, blank], axis=0)
        highs.append(full.astype(jnp.bfloat16))
        lows.append((full - highs[-1].astype(jnp.float32)).astype(jnp.bfloat16))
    pairs = jnp.concatenate([jnp.concatenate([h, l], axis=1) for h, l in zip(highs, lows)], axis=0)
    along_lanes = jnp.dot(pairs, lanes_matrix, preferred_element_type=jnp.float32)
    along_rows = []
    for at in range(0, count, 2):
        high_row, low_row = jnp.concatenate(highs[at : at + 2], axis=1), jnp.concatenate(lows[at : at + 2], axis=1)
        stacked = jnp.concatenate([high_row, low_row, high_row], axis=0)
        along_rows.append(jnp.dot(rows_matrix, stacked, preferred_element_type=jnp.float32))
    along_rows = jnp.concatenate(along_rows, axis=1)
    turned = [
        [t if k == 0 else pltpu.roll(t, NZ * k, 1) for k in range(LANES // NZ)] for t in tiles
    ]
    result = []
    for t, tile in enumerate(tiles):
        total = diagonal[t] * tile
        for (away, turn), factor in couplings.items():
            if 0 <= t + away < count:
                total = total + factor * turned[t + away][turn]
        lanes_part = along_lanes[t * padded : t * padded + height]
        rows_part = along_rows[:height, t * LANES : (t + 1) * LANES]
        result.append(total + (rows_part + (lanes_part[:, :LANES] + lanes_part[:, LANES:])))
    return result


def looked_up(pattern, index):
    if isinstance(index, int):
        return pattern[index]
    value = jnp.zeros_like(index)
    for at, entry in enumerate(pattern):
        value = jnp.where(index == at, entry, value)
    return value


def reordered(place, size, pattern):
    length = len(pattern)
    if size % length:
        return place
    return place // length * length + looked_up(pattern, place % length)


def device_at(place, st, gr):
    return reordered(place // gr, st, st_pattern) * gr + reordered(place % gr, gr, gr_pattern)


def filter_kernel(
    st, gr, slab,
    state_hbm, regions_hbm, table_hbm, order_hbm, subspace_hbm,
    out_ref, weights_ref,
    state_ref, regions_ref, table_ref, order_ref, subspace_ref, lanes_ref, sems,
):
    sources = (order_hbm, subspace_hbm, table_hbm, regions_hbm, state_hbm)
    targets = (order_ref, subspace_ref, table_ref, regions_ref, state_ref)
    copies = [pltpu.make_async_copy(a, b, sems.at[i]) for i, (a, b) in enumerate(zip(sources, targets))]
    for copy in copies:
        copy.start()
    height, width = regions_ref.shape
    count = width // LANES
    levels = table_ref.shape[0]
    shape = (height, LANES)
    high = in_tile_matrix(0)
    lanes_ref[:LANES, :LANES] = high
    lanes_ref[LANES:, :LANES] = high
    lanes_ref[:LANES, LANES:] = in_tile_matrix(1)
    lanes_ref[LANES:, LANES:] = jnp.zeros((LANES, LANES), jnp.bfloat16)
    rows_matrix = row_matrix(height, -(-height // 16) * 16)
    couplings = tile_couplings(shape)
    copies[0].wait()
    copies[1].wait()
    columns, states = subspace_ref.shape
    place = lax.broadcasted_iota(jnp.int32, (states, states), 0)
    here = lax.broadcasted_iota(jnp.int32, (states, states), 1)
    chosen = jnp.where(order_ref[...] == place, 1.0, 0.0).astype(jnp.bfloat16)
    weights = jnp.dot(subspace_ref[...], chosen, preferred_element_type=jnp.float32)
    ones = jnp.ones((states, LANES), jnp.bfloat16)
    for j in range(columns):
        spread = jnp.where(device_at(place, st, gr) == here, weights[j : j + 1], 0.0).astype(jnp.bfloat16)
        weights_ref[j] = jnp.dot(spread, ones, preferred_element_type=jnp.float32)
    diagonal = []
    copies[2].wait()
    copies[3].wait()
    for t in range(count):
        region = regions_ref[:, t * LANES : (t + 1) * LANES]
        potential = jnp.zeros(shape, jnp.float32)
        for level in range(levels):
            potential = jnp.where(region == level, table_ref[level], potential)
        diagonal.append((potential - (centre + 1.5 * coef_center)) * (1.0 / half_width))
    copies[4].wait()
    previous = [state_ref[0, :, t * LANES : (t + 1) * LANES] for t in range(count)]
    current = scaled_op(previous, diagonal, rows_matrix, lanes_ref[...], couplings)
    for _ in range(1, DEG):
        applied = scaled_op(current, diagonal, rows_matrix, lanes_ref[...], couplings)
        following = [2.0 * a - p for a, p in zip(applied, previous)]
        previous, current = current, following
    slabs = [device_at(place, st, gr) % gr for place in range(gr)]
    pieces = [tile[g * slab : (g + 1) * slab] for g in slabs for tile in current]
    filtered = jnp.concatenate(pieces, axis=0).astype(jnp.bfloat16)
    size = filtered.shape[0]

    def put(copy, _):
        out_ref[pl.ds(pl.multiple_of(copy * size, 16), size)] = filtered
        return _

    copies_out = out_ref.shape[0] // size
    lax.fori_loop(0, copies_out, put, 0, unroll=math.gcd(copies_out, 8))


def rotate_kernel(weights_ref, blocks_ref, out_ref):
    states = weights_ref.shape[1]
    slab, columns, width = out_ref.shape
    rows = slab * width // LANES
    pair = 2 * rows
    sublane = lax.broadcasted_iota(jnp.int32, (8, LANES), 0)

    def body(p, totals):
        tiles = [
            blocks_ref[pl.ds(pl.multiple_of(p * pair + 8 * i, 8), 8)].astype(jnp.float32) for i in range(pair // 8)
        ]
        result = []
        for j in range(columns):
            first = jnp.broadcast_to(weights_ref[j, pl.ds(2 * p, 1)], (8, LANES))
            second = jnp.broadcast_to(weights_ref[j, pl.ds(2 * p + 1, 1)], (8, LANES))
            for i, tile in enumerate(tiles):
                if 8 * i + 8 <= rows:
                    weight = first
                elif 8 * i >= rows:
                    weight = second
                else:
                    weight = jnp.where(sublane < rows - 8 * i, first, second)
                result.append(totals[len(result)] + weight * tile)
        return tuple(result)

    start = tuple(jnp.zeros((8, LANES), jnp.float32) for _ in range(columns * pair // 8))
    totals = lax.fori_loop(0, states // 2, body, start, unroll=8 if states % 16 == 0 else 1)
    for j in range(columns):
        both = jnp.concatenate(totals[j * (pair // 8) : (j + 1) * (pair // 8)], axis=0)
        total = both[:rows] + both[rows:]
        for t in range(width // LANES):
            out_ref[:, j, t * LANES : (t + 1) * LANES] = total[t * slab : (t + 1) * slab].astype(out_ref.dtype)


def grant(array):
    return 3 * array.size * array.dtype.itemsize + (4 << 20)


def per_device(st, gr, states, regions, pot_table, subspace, state_order):
    height, width = regions.shape
    slab = height // gr
    rows = slab * width // LANES
    columns = subspace.shape[1]
    hbm = pl.BlockSpec(memory_space=pltpu.HBM)
    vmem = pl.BlockSpec(memory_space=pltpu.VMEM)
    unit = math.gcd(rows, 8)
    chunk = (rows // unit, unit, LANES)
    filtered = jax.ShapeDtypeStruct((st * gr * rows, LANES), jnp.bfloat16)
    order = state_order.reshape(1, -1)
    inputs = [pltpu.with_memory_space_constraint(a, pltpu.HBM) for a in (states, regions, pot_table, order, subspace.T)]
    spaces = (pltpu.VMEM, pltpu.VMEM, pltpu.SMEM, pltpu.VMEM, pltpu.VMEM)
    outgoing, weights = pl.pallas_call(
        functools.partial(filter_kernel, st, gr, slab),
        out_shape=(filtered, jax.ShapeDtypeStruct((columns, subspace.shape[0], LANES), jnp.float32)),
        in_specs=[hbm] * 5,
        out_specs=(vmem, vmem),
        scratch_shapes=[space(a.shape, a.dtype) for space, a in zip(spaces, inputs)]
        + [pltpu.VMEM((2 * LANES, 2 * LANES), jnp.bfloat16), pltpu.SemaphoreType.DMA((5,))],
        compiler_params=pltpu.CompilerParams(vmem_limit_bytes=grant(filtered)),
    )(*inputs)
    blocks = lax.all_to_all(
        outgoing.reshape(st * gr, *chunk),
        ("st", "gr"),
        split_axis=0,
        concat_axis=0,
        tiled=True,
        axis_index_groups=[[device_at(place, st, gr) for place in range(st * gr)]],
    )
    rotated = pl.pallas_call(
        rotate_kernel,
        out_shape=jax.ShapeDtypeStruct((slab, columns, width), jnp.bfloat16),
        in_specs=[vmem, vmem],
        out_specs=vmem,
        compiler_params=pltpu.CompilerParams(vmem_limit_bytes=grant(blocks)),
    )(weights, blocks.reshape(-1, LANES))
    return rotated.transpose(1, 0, 2)


def solution(mesh):
    in_specs = (P(("st", "gr"), None, None), P(), P(), P(None, "st"), P())
    out_specs = P("st", "gr", None)
    body = functools.partial(per_device, mesh.shape["st"], mesh.shape["gr"])
    return jax.shard_map(body, mesh=mesh, in_specs=in_specs, out_specs=out_specs, check_vma=False)
```

```python
import functools
import math

import jax
import jax.numpy as jnp
import numpy as np
from jax import lax
from jax.experimental import pallas as pl
from jax.experimental.pallas import tpu as pltpu
from jax.sharding import PartitionSpec as P

NZ = 32
DEG = 4
LANES = 128

coef_center = -5369.0 / 1800.0
coef_list = (12.0 / 7.0, -15.0 / 56.0, 10.0 / 189.0, -1.0 / 112.0, 2.0 / 1925.0, -1.0 / 16632.0)
centre = 6.75
half_width = 5.25

st_pattern = (6, 2, 0, 4, 3, 7, 1, 5)
gr_pattern = (0, 2, 3, 1)


weight_list = tuple(-0.5 * c / half_width for c in coef_list)


def halves(level):
    high = float(np.float32(weight_list[level]).astype(jnp.bfloat16))
    return high, weight_list[level] - high


def banded(distance, allowed, part):
    matrix = jnp.zeros(distance.shape, jnp.float32)
    for level in range(len(weight_list)):
        matrix = jnp.where(distance == level + 1, halves(level)[part], matrix)
    return jnp.where(allowed, matrix, 0.0).astype(jnp.bfloat16)


def in_tile_matrix(part):
    shape = (LANES, LANES)
    source = lax.broadcasted_iota(jnp.int32, shape, 0)
    target = lax.broadcasted_iota(jnp.int32, shape, 1)
    along_z = banded(abs(source - target), source // NZ == target // NZ, part)
    along_y = banded(abs(source // NZ - target // NZ), source % NZ == target % NZ, part)
    return along_z + along_y


def row_matrix(height, padded):
    shape = (padded, padded)
    target = lax.broadcasted_iota(jnp.int32, shape, 0)
    source = lax.broadcasted_iota(jnp.int32, shape, 1)
    high, low = (banded(abs(source - target), source < height, part) for part in (0, 1))
    return jnp.concatenate([high, high, low], axis=1)


def tile_couplings(shape):
    group = lax.broadcasted_iota(jnp.int32, shape, 1) // NZ
    per_tile, reach = LANES // NZ, len(weight_list)
    couplings = {}
    for away in range(-(reach // per_tile) - 1, reach // per_tile + 2):
        if away == 0:
            continue
        for turn in range(per_tile):
            steps = [abs(per_tile * away + (g - turn) % per_tile - g) for g in range(per_tile)]
            if min(steps) > reach:
                continue
            factor = jnp.zeros(shape, jnp.float32)
            for g, step in enumerate(steps):
                if step <= reach:
                    factor = jnp.where(group == g, weight_list[step - 1], factor)
            couplings[away, turn] = factor
    return couplings


def scaled_op(tiles, diagonal, rows_matrix, lanes_matrix, couplings):
    count = len(tiles)
    height = tiles[0].shape[0]
    padded = rows_matrix.shape[0]
    blank = jnp.zeros((padded - height, LANES), jnp.float32)
    highs, lows = [], []
    for tile in tiles:
        full = jnp.concatenate([tile, blank], axis=0)
        highs.append(full.astype(jnp.bfloat16))
        lows.append((full - highs[-1].astype(jnp.float32)).astype(jnp.bfloat16))
    pairs = jnp.concatenate([jnp.concatenate([h, l], axis=1) for h, l in zip(highs, lows)], axis=0)
    along_lanes = jnp.dot(pairs, lanes_matrix, preferred_element_type=jnp.float32)
    along_rows = []
    for at in range(0, count, 2):
        high_row, low_row = jnp.concatenate(highs[at : at + 2], axis=1), jnp.concatenate(lows[at : at + 2], axis=1)
        stacked = jnp.concatenate([high_row, low_row, high_row], axis=0)
        along_rows.append(jnp.dot(rows_matrix, stacked, preferred_element_type=jnp.float32))
    along_rows = jnp.concatenate(along_rows, axis=1)
    turned = [
        [t if k == 0 else pltpu.roll(t, NZ * k, 1) for k in range(LANES // NZ)] for t in tiles
    ]
    result = []
    for t, tile in enumerate(tiles):
        total = diagonal[t] * tile
        for (away, turn), factor in couplings.items():
            if 0 <= t + away < count:
                total = total + factor * turned[t + away][turn]
        lanes_part = along_lanes[t * padded : t * padded + height]
        rows_part = along_rows[:height, t * LANES : (t + 1) * LANES]
        result.append(total + (rows_part + (lanes_part[:, :LANES] + lanes_part[:, LANES:])))
    return result


def looked_up(pattern, index):
    if isinstance(index, int):
        return pattern[index]
    value = jnp.zeros_like(index)
    for at, entry in enumerate(pattern):
        value = jnp.where(index == at, entry, value)
    return value


def reordered(place, size, pattern):
    length = len(pattern)
    if size % length:
        return place
    return place // length * length + looked_up(pattern, place % length)


def device_at(place, st, gr):
    return reordered(place // gr, st, st_pattern) * gr + reordered(place % gr, gr, gr_pattern)


def filter_kernel(
    st, gr, slab,
    state_hbm, regions_hbm, table_hbm, order_hbm, subspace_hbm,
    out_ref, weights_ref,
    state_ref, regions_ref, table_ref, order_ref, subspace_ref, lanes_ref, sems,
):
    sources = (order_hbm, subspace_hbm, table_hbm, regions_hbm, state_hbm)
    targets = (order_ref, subspace_ref, table_ref, regions_ref, state_ref)
    copies = [pltpu.make_async_copy(a, b, sems.at[i]) for i, (a, b) in enumerate(zip(sources, targets))]
    for copy in copies[::-1]:
        copy.start()
    height, width = regions_ref.shape
    count = width // LANES
    levels = table_ref.shape[0]
    shape = (height, LANES)
    high = in_tile_matrix(0)
    lanes_ref[:LANES, :LANES] = high
    lanes_ref[LANES:, :LANES] = high
    lanes_ref[:LANES, LANES:] = in_tile_matrix(1)
    lanes_ref[LANES:, LANES:] = jnp.zeros((LANES, LANES), jnp.bfloat16)
    rows_matrix = row_matrix(height, -(-height // 16) * 16)
    couplings = tile_couplings(shape)
    copies[0].wait()
    copies[1].wait()
    columns, states = subspace_ref.shape
    place = lax.broadcasted_iota(jnp.int32, (states, states), 0)
    here = lax.broadcasted_iota(jnp.int32, (states, states), 1)
    chosen = jnp.where(order_ref[...] == place, 1.0, 0.0).astype(jnp.bfloat16)
    weights = jnp.dot(subspace_ref[...], chosen, preferred_element_type=jnp.float32)
    ones = jnp.ones((states, LANES), jnp.bfloat16)
    for j in range(columns):
        spread = jnp.where(device_at(place, st, gr) == here, weights[j : j + 1], 0.0).astype(jnp.bfloat16)
        weights_ref[j] = jnp.dot(spread, ones, preferred_element_type=jnp.float32)
    diagonal = []
    copies[2].wait()
    copies[3].wait()
    for t in range(count):
        region = regions_ref[:, t * LANES : (t + 1) * LANES]
        potential = jnp.zeros(shape, jnp.float32)
        for level in range(levels):
            potential = jnp.where(region == level, table_ref[level], potential)
        diagonal.append((potential - (centre + 1.5 * coef_center)) * (1.0 / half_width))
    copies[4].wait()
    previous = [state_ref[0, :, t * LANES : (t + 1) * LANES] for t in range(count)]
    current = scaled_op(previous, diagonal, rows_matrix, lanes_ref[...], couplings)
    for _ in range(1, DEG):
        applied = scaled_op(current, diagonal, rows_matrix, lanes_ref[...], couplings)
        following = [2.0 * a - p for a, p in zip(applied, previous)]
        previous, current = current, following
    slabs = [device_at(place, st, gr) % gr for place in range(gr)]
    pieces = [tile[g * slab : (g + 1) * slab] for g in slabs for tile in current]
    filtered = jnp.concatenate(pieces, axis=0).astype(jnp.bfloat16)
    size = filtered.shape[0]

    def put(copy, _):
        out_ref[pl.ds(pl.multiple_of(copy * size, 16), size)] = filtered
        return _

    copies_out = out_ref.shape[0] // size
    lax.fori_loop(0, copies_out, put, 0, unroll=math.gcd(copies_out, 8))


def rotate_kernel(weights_ref, blocks_ref, out_ref):
    states = weights_ref.shape[1]
    slab, columns, width = out_ref.shape
    rows = slab * width // LANES
    pair = 2 * rows
    sublane = lax.broadcasted_iota(jnp.int32, (8, LANES), 0)

    def body(p, totals):
        tiles = [
            blocks_ref[pl.ds(pl.multiple_of(p * pair + 8 * i, 8), 8)].astype(jnp.float32) for i in range(pair // 8)
        ]
        result = []
        for j in range(columns):
            first = jnp.broadcast_to(weights_ref[j, pl.ds(2 * p, 1)], (8, LANES))
            second = jnp.broadcast_to(weights_ref[j, pl.ds(2 * p + 1, 1)], (8, LANES))
            for i, tile in enumerate(tiles):
                if 8 * i + 8 <= rows:
                    weight = first
                elif 8 * i >= rows:
                    weight = second
                else:
                    weight = jnp.where(sublane < rows - 8 * i, first, second)
                result.append(totals[len(result)] + weight * tile)
        return tuple(result)

    start = tuple(jnp.zeros((8, LANES), jnp.float32) for _ in range(columns * pair // 8))
    totals = lax.fori_loop(0, states // 2, body, start, unroll=8 if states % 16 == 0 else 1)
    for j in range(columns):
        both = jnp.concatenate(totals[j * (pair // 8) : (j + 1) * (pair // 8)], axis=0)
        total = both[:rows] + both[rows:]
        for t in range(width // LANES):
            out_ref[:, j, t * LANES : (t + 1) * LANES] = total[t * slab : (t + 1) * slab].astype(out_ref.dtype)


def grant(array):
    return 3 * array.size * array.dtype.itemsize + (4 << 20)


def per_device(st, gr, states, regions, pot_table, subspace, state_order):
    height, width = regions.shape
    slab = height // gr
    rows = slab * width // LANES
    columns = subspace.shape[1]
    hbm = pl.BlockSpec(memory_space=pltpu.HBM)
    vmem = pl.BlockSpec(memory_space=pltpu.VMEM)
    unit = math.gcd(rows, 8)
    chunk = (rows // unit, unit, LANES)
    filtered = jax.ShapeDtypeStruct((st * gr * rows, LANES), jnp.bfloat16)
    order = state_order.reshape(1, -1)
    inputs = [pltpu.with_memory_space_constraint(a, pltpu.HBM) for a in (states, regions, pot_table, order, subspace.T)]
    spaces = (pltpu.VMEM, pltpu.VMEM, pltpu.SMEM, pltpu.VMEM, pltpu.VMEM)
    outgoing, weights = pl.pallas_call(
        functools.partial(filter_kernel, st, gr, slab),
        out_shape=(filtered, jax.ShapeDtypeStruct((columns, subspace.shape[0], LANES), jnp.float32)),
        in_specs=[hbm] * 5,
        out_specs=(vmem, vmem),
        scratch_shapes=[space(a.shape, a.dtype) for space, a in zip(spaces, inputs)]
        + [pltpu.VMEM((2 * LANES, 2 * LANES), jnp.bfloat16), pltpu.SemaphoreType.DMA((5,))],
        compiler_params=pltpu.CompilerParams(vmem_limit_bytes=grant(filtered)),
    )(*inputs)
    blocks = lax.all_to_all(
        outgoing.reshape(st * gr, *chunk),
        ("st", "gr"),
        split_axis=0,
        concat_axis=0,
        tiled=True,
        axis_index_groups=[[device_at(place, st, gr) for place in range(st * gr)]],
    )
    rotated = pl.pallas_call(
        rotate_kernel,
        out_shape=jax.ShapeDtypeStruct((slab, columns, width), jnp.bfloat16),
        in_specs=[vmem, vmem],
        out_specs=vmem,
        compiler_params=pltpu.CompilerParams(vmem_limit_bytes=grant(blocks)),
    )(weights, blocks.reshape(-1, LANES))
    return rotated.transpose(1, 0, 2)


def solution(mesh):
    in_specs = (P(("st", "gr"), None, None), P(), P(), P(None, "st"), P())
    out_specs = P("st", "gr", None)
    body = functools.partial(per_device, mesh.shape["st"], mesh.shape["gr"])
    return jax.shard_map(body, mesh=mesh, in_specs=in_specs, out_specs=out_specs, check_vma=False)
```

```python
import functools
import math

import jax
import jax.numpy as jnp
import numpy as np
from jax import lax
from jax.experimental import pallas as pl
from jax.experimental.pallas import tpu as pltpu
from jax.sharding import PartitionSpec as P

NZ = 32
DEG = 4
LANES = 128

coef_center = -5369.0 / 1800.0
coef_list = (12.0 / 7.0, -15.0 / 56.0, 10.0 / 189.0, -1.0 / 112.0, 2.0 / 1925.0, -1.0 / 16632.0)
centre = 6.75
half_width = 5.25

st_pattern = (7, 3, 5, 6, 2, 0, 4, 1)
gr_pattern = (0, 2, 3, 1)


weight_list = tuple(-0.5 * c / half_width for c in coef_list)


def halves(level):
    high = float(np.float32(weight_list[level]).astype(jnp.bfloat16))
    return high, weight_list[level] - high


def banded(distance, allowed, part):
    matrix = jnp.zeros(distance.shape, jnp.float32)
    for level in range(len(weight_list)):
        matrix = jnp.where(distance == level + 1, halves(level)[part], matrix)
    return jnp.where(allowed, matrix, 0.0).astype(jnp.bfloat16)


def in_tile_matrix(part):
    shape = (LANES, LANES)
    source = lax.broadcasted_iota(jnp.int32, shape, 0)
    target = lax.broadcasted_iota(jnp.int32, shape, 1)
    along_z = banded(abs(source - target), source // NZ == target // NZ, part)
    along_y = banded(abs(source // NZ - target // NZ), source % NZ == target % NZ, part)
    return along_z + along_y


def row_matrix(height, padded):
    shape = (padded, padded)
    target = lax.broadcasted_iota(jnp.int32, shape, 0)
    source = lax.broadcasted_iota(jnp.int32, shape, 1)
    high, low = (banded(abs(source - target), source < height, part) for part in (0, 1))
    return jnp.concatenate([high, high, low], axis=1)


def tile_couplings(shape):
    group = lax.broadcasted_iota(jnp.int32, shape, 1) // NZ
    per_tile, reach = LANES // NZ, len(weight_list)
    couplings = {}
    for away in range(-(reach // per_tile) - 1, reach // per_tile + 2):
        if away == 0:
            continue
        for turn in range(per_tile):
            steps = [abs(per_tile * away + (g - turn) % per_tile - g) for g in range(per_tile)]
            if min(steps) > reach:
                continue
            factor = jnp.zeros(shape, jnp.float32)
            for g, step in enumerate(steps):
                if step <= reach:
                    factor = jnp.where(group == g, weight_list[step - 1], factor)
            couplings[away, turn] = factor
    return couplings


def scaled_op(tiles, diagonal, rows_matrix, lanes_matrix, couplings):
    count = len(tiles)
    height = tiles[0].shape[0]
    padded = rows_matrix.shape[0]
    blank = jnp.zeros((padded - height, LANES), jnp.float32)
    highs, lows = [], []
    for tile in tiles:
        full = jnp.concatenate([tile, blank], axis=0)
        highs.append(full.astype(jnp.bfloat16))
        lows.append((full - highs[-1].astype(jnp.float32)).astype(jnp.bfloat16))
    pairs = jnp.concatenate([jnp.concatenate([h, l], axis=1) for h, l in zip(highs, lows)], axis=0)
    along_lanes = jnp.dot(pairs, lanes_matrix, preferred_element_type=jnp.float32)
    along_rows = []
    for at in range(0, count, 2):
        high_row, low_row = jnp.concatenate(highs[at : at + 2], axis=1), jnp.concatenate(lows[at : at + 2], axis=1)
        stacked = jnp.concatenate([high_row, low_row, high_row], axis=0)
        along_rows.append(jnp.dot(rows_matrix, stacked, preferred_element_type=jnp.float32))
    along_rows = jnp.concatenate(along_rows, axis=1)
    turned = [
        [t if k == 0 else pltpu.roll(t, NZ * k, 1) for k in range(LANES // NZ)] for t in tiles
    ]
    result = []
    for t, tile in enumerate(tiles):
        total = diagonal[t] * tile
        for (away, turn), factor in couplings.items():
            if 0 <= t + away < count:
                total = total + factor * turned[t + away][turn]
        lanes_part = along_lanes[t * padded : t * padded + height]
        rows_part = along_rows[:height, t * LANES : (t + 1) * LANES]
        result.append(total + (rows_part + (lanes_part[:, :LANES] + lanes_part[:, LANES:])))
    return result


def looked_up(pattern, index):
    if isinstance(index, int):
        return pattern[index]
    value = jnp.zeros_like(index)
    for at, entry in enumerate(pattern):
        value = jnp.where(index == at, entry, value)
    return value


def reordered(place, size, pattern):
    length = len(pattern)
    if size % length:
        return place
    return place // length * length + looked_up(pattern, place % length)


def device_at(place, st, gr):
    return reordered(place // gr, st, st_pattern) * gr + reordered(place % gr, gr, gr_pattern)


def filter_kernel(
    st, gr, slab,
    state_hbm, regions_hbm, table_hbm, order_hbm, subspace_hbm,
    out_ref, weights_ref,
    state_ref, regions_ref, table_ref, order_ref, subspace_ref, lanes_ref, sems,
):
    sources = (order_hbm, subspace_hbm, table_hbm, regions_hbm, state_hbm)
    targets = (order_ref, subspace_ref, table_ref, regions_ref, state_ref)
    copies = [pltpu.make_async_copy(a, b, sems.at[i]) for i, (a, b) in enumerate(zip(sources, targets))]
    for copy in copies[::-1]:
        copy.start()
    height, width = regions_ref.shape
    count = width // LANES
    levels = table_ref.shape[0]
    shape = (height, LANES)
    high = in_tile_matrix(0)
    lanes_ref[:LANES, :LANES] = high
    lanes_ref[LANES:, :LANES] = high
    lanes_ref[:LANES, LANES:] = in_tile_matrix(1)
    lanes_ref[LANES:, LANES:] = jnp.zeros((LANES, LANES), jnp.bfloat16)
    rows_matrix = row_matrix(height, -(-height // 16) * 16)
    couplings = tile_couplings(shape)
    copies[0].wait()
    copies[1].wait()
    columns, states = subspace_ref.shape
    place = lax.broadcasted_iota(jnp.int32, (states, states), 0)
    here = lax.broadcasted_iota(jnp.int32, (states, states), 1)
    chosen = jnp.where(order_ref[...] == place, 1.0, 0.0).astype(jnp.bfloat16)
    weights = jnp.dot(subspace_ref[...], chosen, preferred_element_type=jnp.float32)
    ones = jnp.ones((states, LANES), jnp.bfloat16)
    for j in range(columns):
        spread = jnp.where(device_at(place, st, gr) == here, weights[j : j + 1], 0.0).astype(jnp.bfloat16)
        weights_ref[j] = jnp.dot(spread, ones, preferred_element_type=jnp.float32)
    diagonal = []
    copies[2].wait()
    copies[3].wait()
    for t in range(count):
        region = regions_ref[:, t * LANES : (t + 1) * LANES]
        potential = jnp.zeros(shape, jnp.float32)
        for level in range(levels):
            potential = jnp.where(region == level, table_ref[level], potential)
        diagonal.append((potential - (centre + 1.5 * coef_center)) * (1.0 / half_width))
    copies[4].wait()
    previous = [state_ref[0, :, t * LANES : (t + 1) * LANES] for t in range(count)]
    current = scaled_op(previous, diagonal, rows_matrix, lanes_ref[...], couplings)
    for _ in range(1, DEG):
        applied = scaled_op(current, diagonal, rows_matrix, lanes_ref[...], couplings)
        following = [2.0 * a - p for a, p in zip(applied, previous)]
        previous, current = current, following
    slabs = [device_at(place, st, gr) % gr for place in range(gr)]
    pieces = [tile[g * slab : (g + 1) * slab] for g in slabs for tile in current]
    filtered = jnp.concatenate(pieces, axis=0).astype(jnp.bfloat16)
    size = filtered.shape[0]

    def put(copy, _):
        out_ref[pl.ds(pl.multiple_of(copy * size, 16), size)] = filtered
        return _

    copies_out = out_ref.shape[0] // size
    lax.fori_loop(0, copies_out, put, 0, unroll=math.gcd(copies_out, 8))


def rotate_kernel(weights_ref, blocks_ref, out_ref):
    states = weights_ref.shape[1]
    slab, columns, width = out_ref.shape
    rows = slab * width // LANES
    pair = 2 * rows
    sublane = lax.broadcasted_iota(jnp.int32, (8, LANES), 0)

    def body(p, totals):
        tiles = [
            blocks_ref[pl.ds(pl.multiple_of(p * pair + 8 * i, 8), 8)].astype(jnp.float32) for i in range(pair // 8)
        ]
        result = []
        for j in range(columns):
            first = jnp.broadcast_to(weights_ref[j, pl.ds(2 * p, 1)], (8, LANES))
            second = jnp.broadcast_to(weights_ref[j, pl.ds(2 * p + 1, 1)], (8, LANES))
            for i, tile in enumerate(tiles):
                if 8 * i + 8 <= rows:
                    weight = first
                elif 8 * i >= rows:
                    weight = second
                else:
                    weight = jnp.where(sublane < rows - 8 * i, first, second)
                result.append(totals[len(result)] + weight * tile)
        return tuple(result)

    start = tuple(jnp.zeros((8, LANES), jnp.float32) for _ in range(columns * pair // 8))
    totals = lax.fori_loop(0, states // 2, body, start, unroll=8 if states % 16 == 0 else 1)
    for j in range(columns):
        both = jnp.concatenate(totals[j * (pair // 8) : (j + 1) * (pair // 8)], axis=0)
        total = both[:rows] + both[rows:]
        for t in range(width // LANES):
            out_ref[:, j, t * LANES : (t + 1) * LANES] = total[t * slab : (t + 1) * slab].astype(out_ref.dtype)


def grant(array):
    return 3 * array.size * array.dtype.itemsize + (4 << 20)


def per_device(st, gr, states, regions, pot_table, subspace, state_order):
    height, width = regions.shape
    slab = height // gr
    rows = slab * width // LANES
    columns = subspace.shape[1]
    hbm = pl.BlockSpec(memory_space=pltpu.HBM)
    vmem = pl.BlockSpec(memory_space=pltpu.VMEM)
    unit = math.gcd(rows, 8)
    chunk = (rows // unit, unit, LANES)
    filtered = jax.ShapeDtypeStruct((st * gr * rows, LANES), jnp.bfloat16)
    order = state_order.reshape(1, -1)
    inputs = [pltpu.with_memory_space_constraint(a, pltpu.HBM) for a in (states, regions, pot_table, order, subspace.T)]
    spaces = (pltpu.VMEM, pltpu.VMEM, pltpu.SMEM, pltpu.VMEM, pltpu.VMEM)
    outgoing, weights = pl.pallas_call(
        functools.partial(filter_kernel, st, gr, slab),
        out_shape=(filtered, jax.ShapeDtypeStruct((columns, subspace.shape[0], LANES), jnp.float32)),
        in_specs=[hbm] * 5,
        out_specs=(vmem, vmem),
        scratch_shapes=[space(a.shape, a.dtype) for space, a in zip(spaces, inputs)]
        + [pltpu.VMEM((2 * LANES, 2 * LANES), jnp.bfloat16), pltpu.SemaphoreType.DMA((5,))],
        compiler_params=pltpu.CompilerParams(vmem_limit_bytes=grant(filtered)),
    )(*inputs)
    blocks = lax.all_to_all(
        outgoing.reshape(st * gr, *chunk),
        ("st", "gr"),
        split_axis=0,
        concat_axis=0,
        tiled=True,
        axis_index_groups=[[device_at(place, st, gr) for place in range(st * gr)]],
    )
    rotated = pl.pallas_call(
        rotate_kernel,
        out_shape=jax.ShapeDtypeStruct((slab, columns, width), jnp.bfloat16),
        in_specs=[vmem, vmem],
        out_specs=vmem,
        compiler_params=pltpu.CompilerParams(vmem_limit_bytes=grant(blocks)),
    )(weights, blocks.reshape(-1, LANES))
    return rotated.transpose(1, 0, 2)


def solution(mesh):
    in_specs = (P(("st", "gr"), None, None), P(), P(), P(None, "st"), P())
    out_specs = P("st", "gr", None)
    body = functools.partial(per_device, mesh.shape["st"], mesh.shape["gr"])
    return jax.shard_map(body, mesh=mesh, in_specs=in_specs, out_specs=out_specs, check_vma=False)
```

```python
import functools
import math

import jax
import jax.numpy as jnp
import numpy as np
from jax import lax
from jax.experimental import pallas as pl
from jax.experimental.pallas import tpu as pltpu
from jax.sharding import PartitionSpec as P

NZ = 32
DEG = 4
LANES = 128

coef_center = -5369.0 / 1800.0
coef_list = (12.0 / 7.0, -15.0 / 56.0, 10.0 / 189.0, -1.0 / 112.0, 2.0 / 1925.0, -1.0 / 16632.0)
centre = 6.75
half_width = 5.25

st_pattern = (7, 3, 5, 6, 2, 0, 4, 1)
gr_pattern = (0, 2, 3, 1)


weight_list = tuple(-0.5 * c / half_width for c in coef_list)


def halves(level):
    high = float(np.float32(weight_list[level]).astype(jnp.bfloat16))
    return high, weight_list[level] - high


def banded(distance, allowed, part):
    matrix = jnp.zeros(distance.shape, jnp.float32)
    for level in range(len(weight_list)):
        matrix = jnp.where(distance == level + 1, halves(level)[part], matrix)
    return jnp.where(allowed, matrix, 0.0).astype(jnp.bfloat16)


def in_tile_matrix(part):
    shape = (LANES, LANES)
    source = lax.broadcasted_iota(jnp.int32, shape, 0)
    target = lax.broadcasted_iota(jnp.int32, shape, 1)
    along_z = banded(abs(source - target), source // NZ == target // NZ, part)
    along_y = banded(abs(source // NZ - target // NZ), source % NZ == target % NZ, part)
    return along_z + along_y


def row_matrix(height, padded):
    shape = (padded, padded)
    target = lax.broadcasted_iota(jnp.int32, shape, 0)
    source = lax.broadcasted_iota(jnp.int32, shape, 1)
    high, low = (banded(abs(source - target), source < height, part) for part in (0, 1))
    return jnp.concatenate([high, high, low], axis=1)


def tile_couplings(shape):
    group = lax.broadcasted_iota(jnp.int32, shape, 1) // NZ
    per_tile, reach = LANES // NZ, len(weight_list)
    couplings = {}
    for away in range(-(reach // per_tile) - 1, reach // per_tile + 2):
        if away == 0:
            continue
        for turn in range(per_tile):
            steps = [abs(per_tile * away + (g - turn) % per_tile - g) for g in range(per_tile)]
            if min(steps) > reach:
                continue
            factor = jnp.zeros(shape, jnp.float32)
            for g, step in enumerate(steps):
                if step <= reach:
                    factor = jnp.where(group == g, weight_list[step - 1], factor)
            couplings[away, turn] = factor
    return couplings


def scaled_op(tiles, diagonal, rows_matrix, lanes_matrix, couplings):
    count = len(tiles)
    height = tiles[0].shape[0]
    padded = rows_matrix.shape[0]
    blank = jnp.zeros((padded - height, LANES), jnp.float32)
    highs, lows = [], []
    for tile in tiles:
        full = jnp.concatenate([tile, blank], axis=0)
        highs.append(full.astype(jnp.bfloat16))
        lows.append((full - highs[-1].astype(jnp.float32)).astype(jnp.bfloat16))
    pairs = jnp.concatenate([jnp.concatenate([h, l], axis=1) for h, l in zip(highs, lows)], axis=0)
    along_lanes = jnp.dot(pairs, lanes_matrix, preferred_element_type=jnp.float32)
    along_rows = []
    for at in range(0, count, 2):
        high_row, low_row = jnp.concatenate(highs[at : at + 2], axis=1), jnp.concatenate(lows[at : at + 2], axis=1)
        stacked = jnp.concatenate([high_row, low_row, high_row], axis=0)
        along_rows.append(jnp.dot(rows_matrix, stacked, preferred_element_type=jnp.float32))
    along_rows = jnp.concatenate(along_rows, axis=1)
    turned = [
        [t if k == 0 else pltpu.roll(t, NZ * k, 1) for k in range(LANES // NZ)] for t in tiles
    ]
    result = []
    for t, tile in enumerate(tiles):
        total = diagonal[t] * tile
        for (away, turn), factor in couplings.items():
            if 0 <= t + away < count:
                total = total + factor * turned[t + away][turn]
        lanes_part = along_lanes[t * padded : t * padded + height]
        rows_part = along_rows[:height, t * LANES : (t + 1) * LANES]
        result.append(total + (rows_part + (lanes_part[:, :LANES] + lanes_part[:, LANES:])))
    return result


def looked_up(pattern, index):
    if isinstance(index, int):
        return pattern[index]
    value = jnp.zeros_like(index)
    for at, entry in enumerate(pattern):
        value = jnp.where(index == at, entry, value)
    return value


def reordered(place, size, pattern):
    length = len(pattern)
    if size % length:
        return place
    return place // length * length + looked_up(pattern, place % length)


def device_at(place, st, gr):
    return reordered(place // gr, st, st_pattern) * gr + reordered(place % gr, gr, gr_pattern)


def filter_kernel(
    st, gr, slab,
    state_hbm, regions_hbm, table_hbm, order_hbm, subspace_hbm,
    out_ref, weights_ref,
    state_ref, regions_ref, table_ref, order_ref, subspace_ref, lanes_ref, sems,
):
    sources = (order_hbm, subspace_hbm, table_hbm, regions_hbm, state_hbm)
    targets = (order_ref, subspace_ref, table_ref, regions_ref, state_ref)
    copies = [pltpu.make_async_copy(a, b, sems.at[i]) for i, (a, b) in enumerate(zip(sources, targets))]
    for copy in copies:
        copy.start()
    height, width = regions_ref.shape
    count = width // LANES
    levels = table_ref.shape[0]
    shape = (height, LANES)
    high = in_tile_matrix(0)
    lanes_ref[:LANES, :LANES] = high
    lanes_ref[LANES:, :LANES] = high
    lanes_ref[:LANES, LANES:] = in_tile_matrix(1)
    lanes_ref[LANES:, LANES:] = jnp.zeros((LANES, LANES), jnp.bfloat16)
    rows_matrix = row_matrix(height, -(-height // 16) * 16)
    couplings = tile_couplings(shape)
    copies[0].wait()
    copies[1].wait()
    columns, states = subspace_ref.shape
    place = lax.broadcasted_iota(jnp.int32, (states, states), 0)
    here = lax.broadcasted_iota(jnp.int32, (states, states), 1)
    chosen = jnp.where(order_ref[...] == place, 1.0, 0.0).astype(jnp.bfloat16)
    weights = jnp.dot(subspace_ref[...], chosen, preferred_element_type=jnp.float32)
    ones = jnp.ones((states, LANES), jnp.bfloat16)
    for j in range(columns):
        spread = jnp.where(device_at(place, st, gr) == here, weights[j : j + 1], 0.0).astype(jnp.bfloat16)
        weights_ref[j] = jnp.dot(spread, ones, preferred_element_type=jnp.float32)
    diagonal = []
    copies[2].wait()
    copies[3].wait()
    for t in range(count):
        region = regions_ref[:, t * LANES : (t + 1) * LANES]
        potential = jnp.zeros(shape, jnp.float32)
        for level in range(levels):
            potential = jnp.where(region == level, table_ref[level], potential)
        diagonal.append((potential - (centre + 1.5 * coef_center)) * (1.0 / half_width))
    copies[4].wait()
    previous = [state_ref[0, :, t * LANES : (t + 1) * LANES] for t in range(count)]
    current = scaled_op(previous, diagonal, rows_matrix, lanes_ref[...], couplings)
    for _ in range(1, DEG):
        applied = scaled_op(current, diagonal, rows_matrix, lanes_ref[...], couplings)
        following = [2.0 * a - p for a, p in zip(applied, previous)]
        previous, current = current, following
    slabs = [device_at(place, st, gr) % gr for place in range(gr)]
    pieces = [tile[g * slab : (g + 1) * slab] for g in slabs for tile in current]
    filtered = jnp.concatenate(pieces, axis=0).astype(jnp.bfloat16)
    size = filtered.shape[0]

    def put(copy, _):
        out_ref[pl.ds(pl.multiple_of(copy * size, 16), size)] = filtered
        return _

    copies_out = out_ref.shape[0] // size
    lax.fori_loop(0, copies_out, put, 0, unroll=math.gcd(copies_out, 8))


def rotate_kernel(weights_ref, blocks_ref, out_ref):
    states = weights_ref.shape[1]
    slab, columns, width = out_ref.shape
    rows = slab * width // LANES
    pair = 2 * rows
    sublane = lax.broadcasted_iota(jnp.int32, (8, LANES), 0)

    def body(p, totals):
        tiles = [
            blocks_ref[pl.ds(pl.multiple_of(p * pair + 8 * i, 8), 8)].astype(jnp.float32) for i in range(pair // 8)
        ]
        result = []
        for j in range(columns):
            first = jnp.broadcast_to(weights_ref[j, pl.ds(2 * p, 1)], (8, LANES))
            second = jnp.broadcast_to(weights_ref[j, pl.ds(2 * p + 1, 1)], (8, LANES))
            for i, tile in enumerate(tiles):
                if 8 * i + 8 <= rows:
                    weight = first
                elif 8 * i >= rows:
                    weight = second
                else:
                    weight = jnp.where(sublane < rows - 8 * i, first, second)
                result.append(totals[len(result)] + weight * tile)
        return tuple(result)

    start = tuple(jnp.zeros((8, LANES), jnp.float32) for _ in range(columns * pair // 8))
    totals = lax.fori_loop(0, states // 2, body, start, unroll=16 if states % 32 == 0 else 1)
    for j in range(columns):
        both = jnp.concatenate(totals[j * (pair // 8) : (j + 1) * (pair // 8)], axis=0)
        total = both[:rows] + both[rows:]
        for t in range(width // LANES):
            out_ref[:, j, t * LANES : (t + 1) * LANES] = total[t * slab : (t + 1) * slab].astype(out_ref.dtype)


def grant(array):
    return 3 * array.size * array.dtype.itemsize + (4 << 20)


def per_device(st, gr, states, regions, pot_table, subspace, state_order):
    height, width = regions.shape
    slab = height // gr
    rows = slab * width // LANES
    columns = subspace.shape[1]
    hbm = pl.BlockSpec(memory_space=pltpu.HBM)
    vmem = pl.BlockSpec(memory_space=pltpu.VMEM)
    unit = math.gcd(rows, 8)
    chunk = (rows // unit, unit, LANES)
    filtered = jax.ShapeDtypeStruct((st * gr * rows, LANES), jnp.bfloat16)
    order = state_order.reshape(1, -1)
    inputs = [pltpu.with_memory_space_constraint(a, pltpu.HBM) for a in (states, regions, pot_table, order, subspace.T)]
    spaces = (pltpu.VMEM, pltpu.VMEM, pltpu.SMEM, pltpu.VMEM, pltpu.VMEM)
    outgoing, weights = pl.pallas_call(
        functools.partial(filter_kernel, st, gr, slab),
        out_shape=(filtered, jax.ShapeDtypeStruct((columns, subspace.shape[0], LANES), jnp.float32)),
        in_specs=[hbm] * 5,
        out_specs=(vmem, vmem),
        scratch_shapes=[space(a.shape, a.dtype) for space, a in zip(spaces, inputs)]
        + [pltpu.VMEM((2 * LANES, 2 * LANES), jnp.bfloat16), pltpu.SemaphoreType.DMA((5,))],
        compiler_params=pltpu.CompilerParams(vmem_limit_bytes=grant(filtered)),
    )(*inputs)
    blocks = lax.all_to_all(
        outgoing.reshape(st * gr, *chunk),
        ("st", "gr"),
        split_axis=0,
        concat_axis=0,
        tiled=True,
        axis_index_groups=[[device_at(place, st, gr) for place in range(st * gr)]],
    )
    rotated = pl.pallas_call(
        rotate_kernel,
        out_shape=jax.ShapeDtypeStruct((slab, columns, width), jnp.bfloat16),
        in_specs=[vmem, vmem],
        out_specs=vmem,
        compiler_params=pltpu.CompilerParams(vmem_limit_bytes=grant(blocks)),
    )(weights, blocks.reshape(-1, LANES))
    return rotated.transpose(1, 0, 2)


def solution(mesh):
    in_specs = (P(("st", "gr"), None, None), P(), P(), P(None, "st"), P())
    out_specs = P("st", "gr", None)
    body = functools.partial(per_device, mesh.shape["st"], mesh.shape["gr"])
    return jax.shard_map(body, mesh=mesh, in_specs=in_specs, out_specs=out_specs, check_vma=False)
```
